32 devices in a mesh: layer: 4 (over x, core), grid: 8 (over z, y).
Axes of the slice: x: 2, y: 2, z: 4, core: 2. Of those that a mesh axis runs over, the one named last changes fastest.
Arguments:
- band_blocks: bfloat16 [80, 9, 128, 128], P('grid'), may hold values from -7 to 7, as said below
- retained: int32 [80, 9], P('grid'), may hold values from 0 to 1, as said below
Outputs:
- purified: bfloat16 [80, 9, 128, 128], P('grid', None, 'layer')
The draws below stay inside these ranges and needn't reach their ends.
Inputs may be any that keep to these rules, and one draw needn't show every extreme that they name: `band_blocks`: the matrix is symmetric: block slot w of block row i equals the transpose of block slot 8 - w of block row (i + w - 4) mod 80. retained[i, w] = 1 exactly when retained[(i + w - 4) mod 80, 8 - w] = 1; the middle slot w = 4 is 1 in every block row.
All inputs are finite; a program needn't handle non-finite values.
Results may differ from the reference program's by a relative error of at most 0.005.
Values may be sent and summed in bfloat16 or wider, within the bound.
A program may use at most 64 MiB of HBM per device.

```python
import jax
import jax.numpy as jnp
from jax import lax

BLOCK = 128
REACH = 4
BAND = 9
STEPS = 2
NB = 80


def mirror_tables():
    row_table = (jnp.arange(NB)[:, None] + jnp.arange(BAND)[None, :] - REACH) % NB
    slot_table = (BAND - 1 - jnp.arange(BAND))[None, :]
    return (row_table.astype(jnp.int32), slot_table.astype(jnp.int32))


def draw_band_blocks(key, part):
    first_key = jax.random.fold_in(key, 11)
    second_key = jax.random.fold_in(key, 12)
    shape = (NB, BAND, BLOCK, BLOCK)
    base = jnp.clip(jax.random.normal(first_key, shape, jnp.float32), -3.5, 3.5)
    extra = jnp.clip(jax.random.normal(second_key, shape, jnp.float32), -3.5, 3.5)
    row_table, slot_table = mirror_tables()
    mirror = jnp.swapaxes(base[row_table, slot_table], 2, 3)
    extra_mirror = jnp.swapaxes(extra[row_table, slot_table], 2, 3)
    joined = 1.026 * (base + mirror) + 0.57275649 * (extra + extra_mirror)
    return jnp.clip(joined, -7.0, 7.0).astype(jnp.bfloat16)


def draw_retained(key, part):
    coin_key = jax.random.fold_in(key, 21)
    coins = jax.random.randint(coin_key, (NB, BAND), 0, 2).astype(jnp.int32)
    row_table, slot_table = mirror_tables()
    joined = jnp.maximum(coins, coins[row_table, slot_table])
    middle = (jnp.arange(BAND) == REACH)[None, :]
    return jnp.where(middle, 1, joined).astype(jnp.int32)


def setup_inputs(seed: int = 0) -> dict:
    seeds = jax.random.split(jax.random.key(seed), 3)
    return {
        "band_blocks": draw_band_blocks(jax.random.fold_in(seeds[2], 71), 0),
        "retained": draw_retained(jax.random.fold_in(seeds[2], 71), 0),
    }


def band_product(left_blocks, right_blocks):
    left_wide = left_blocks.astype(jnp.float32)
    right_wide = right_blocks.astype(jnp.float32)
    total = jnp.zeros(left_blocks.shape, jnp.float32)
    for offset in range(BAND):
        moved = jnp.roll(right_wide, REACH - offset, axis=0)
        lowest = max(0, offset - REACH)
        highest = min(BAND, BAND + offset - REACH)
        source = moved[:, lowest - offset + REACH:highest - offset + REACH]
        product_term = jnp.einsum('nab,nwbc->nwac', left_wide[:, offset], source, precision=lax.Precision.HIGHEST)
        total = total.at[:, lowest:highest].add(product_term)
    return total


def reference(band_blocks, retained):
    kept = (retained != 0)[:, :, None, None]
    current = jnp.where(kept, band_blocks, jnp.zeros_like(band_blocks))
    for repeat in range(STEPS):
        square = jnp.where(kept, band_product(current, current), 0.0).astype(jnp.bfloat16)
        cube = jnp.where(kept, band_product(square, current), 0.0)
        current = ((3.0 * current.astype(jnp.float32) - cube / (4.0 * BAND * BLOCK)) * 0.5).astype(jnp.bfloat16)
    return current
```

```python
import functools

import jax
import jax.numpy as jnp
from jax import lax
from jax.experimental import pallas as pl
from jax.experimental.pallas import tpu as pltpu
from jax.sharding import PartitionSpec as P

MESH = pl.DeviceIdType.MESH


def purify(dims, x_hbm, r_hbm, o_ref, x_ref, halo, flags, r2, wide, cur, strip, part, part_square,
           outbox, y_send, y_recv, x_send, x_recv, c_send, c_recv, o_send, o_recv, r_send, r_recv,
           local, local_flags):
    layers, grids, rows, reach, block = dims
    piece = block // layers
    pair = 2 * piece
    band = 2 * reach + 1
    depth = 2 * reach
    tile = 2 * block
    span = reach // 2
    half = rows // 2
    scale = 1.0 / (4.0 * band * block)
    last = (depth + half - 1) // 2
    tiles = last + span + 1
    own = reach
    edge = own - span

    q = lax.axis_index("layer")
    g = lax.axis_index("grid")
    core = lax.rem(q, 2)
    base = q - core
    right = lax.rem(g + 1, grids)
    left = lax.rem(g + grids - 1, grids)
    far = lax.rem(q + layers // 2, layers)
    near = base + 1 - core
    outer = jnp.where(core == 0, left, right)
    inner = jnp.where(core == 0, right, left)

    def mirror(i, count):
        return i + core * (count - 1 - 2 * i)

    def strip_of(index, size):
        return pl.ds(pl.multiple_of(index * size, size), size)

    own_flags = pltpu.make_async_copy(r_hbm, r2.at[0], local_flags.at[0])
    own_flags.start()
    order = range(rows)
    own_rows = [
        pltpu.make_async_copy(
            x_hbm.at[mirror(r, rows)], x_ref.at[mirror(r, rows)], local.at[r]
        )
        for r in order
    ]
    for r in order:
        own_rows[r].start()

    barrier = pltpu.get_barrier_semaphore()
    peers = ((base, outer), (base + 1, outer), (far, g), (near, g))
    for peer in peers:
        pl.semaphore_signal(barrier, inc=1, device_id=peer, device_id_type=MESH)

    def remote(source, target, send_sem, recv_sem, peer):
        return pltpu.make_async_remote_copy(
            src_ref=source,
            dst_ref=target,
            send_sem=send_sem,
            recv_sem=recv_sem,
            device_id=peer,
            device_id_type=MESH,
        )

    mine = strip_of(q, piece)
    plane = lax.div(q, 2)
    near_rows = strip_of(plane, pair)
    far_rows = strip_of(lax.div(far, 2), pair)
    sides = ((base, right), (base + 1, left))
    sends = {}
    arrivals = {}
    crossings = {}
    landings = {}
    for j in range(depth):
        count = min(reach + 1, j + 1)
        for side in range(2):
            if side == 0:
                source = x_hbm.at[rows - 1 - j, reach : reach + count, mine, :]
            else:
                source = x_hbm.at[j, reach + 1 - count : reach + 1, mine, :]
            there = halo.at[j, 0:count, mine, :]
            sends[side, j] = remote(
                source, there, y_send.at[side, j], y_recv.at[core, j], sides[side]
            )
        for p in range(2):
            here = halo.at[j, 0:count, strip_of(base + p, piece), :]
            arrivals[p, j] = remote(here, here, y_send.at[p, j], y_recv.at[p, j], (near, g))
        across = halo.at[j, 0:count, near_rows, :]
        crossings[j] = remote(across, across, x_send.at[j], x_recv.at[j], (far, g))
        beyond = halo.at[j, 0:count, far_rows, :]
        landings[j] = remote(beyond, beyond, x_send.at[j], x_recv.at[j], (far, g))
    flag_copy = remote(r_hbm, flags, r_send, r_recv, (q, inner))

    def at(r):
        return slice((r + depth) * block, (r + depth + 1) * block)

    def cur_at(r):
        return slice((r + reach) * block, (r + reach + 1) * block)

    def masked(value, r, w):
        kept = r2[0 if r >= 0 else 1, mirror(r % rows, rows), mirror(w, band)]
        return jnp.where(kept != 0, value, jnp.zeros_like(value))

    def put(r, c, value):
        wide[at(r), at(c)] = value

    empty = jnp.zeros((block, block), jnp.bfloat16)
    blank = jnp.zeros((pair, block), jnp.bfloat16)

    def height(i):
        return min(2, depth + half - 2 * i)

    def extent(i, c):
        return max(i, c) - span, min(i, c) + span + 1

    def squares(i, columns):
        m = height(i)
        lines = slice(i * tile, i * tile + m * block)
        for c in columns:
            low, high = extent(i, c)
            product = jnp.dot(
                wide[lines, low * tile : high * tile],
                wide[low * tile : high * tile, c * tile : (c + 1) * tile],
                preferred_element_type=jnp.float32,
            )
            for a in range(m):
                for b in range(2):
                    w = 2 * (c - i) + b - a + reach
                    if 0 <= w < band:
                        value = masked(
                            product[a * block : (a + 1) * block, b * block : (b + 1) * block],
                            2 * i - depth + a,
                            w,
                        ).astype(jnp.bfloat16)
                    else:
                        value = empty
                    to = (c - i + span) * tile + b * block
                    strip[i - edge, a * block : (a + 1) * block, to : to + block] = value

    def cubes(i, columns):
        m = height(i)
        lines = slice(i * tile, i * tile + m * block)
        for k in columns:
            low, high = extent(i, k)
            product = jnp.dot(
                strip[
                    i - edge, 0 : m * block, (low - i + span) * tile : (high - i + span) * tile
                ],
                wide[low * tile : high * tile, k * tile : (k + 1) * tile],
                preferred_element_type=jnp.float32,
            )
            before = wide[lines, k * tile : (k + 1) * tile].astype(jnp.float32)
            after = (3.0 * before - product * scale) * 0.5
            for a in range(m):
                r = 2 * i - depth + a
                for b in range(2):
                    c = 2 * k - depth + b
                    w = c - r + reach
                    if 0 <= w < band:
                        value = masked(
                            after[a * block : (a + 1) * block, b * block : (b + 1) * block], r, w
                        ).astype(jnp.bfloat16)
                    else:
                        value = empty
                    cur[cur_at(r), cur_at(c)] = value

    def part_at(r):
        return slice(r * pair, (r + 1) * pair)

    def gather(i):
        for a in range(height(i)):
            r = 2 * i - depth + a
            for k in range(i - span, i + span + 1):
                for b in range(2):
                    c = 2 * k - depth + b
                    if abs(c - r) <= reach:
                        for p, layer in enumerate((q, near)):
                            start = (r + reach) * block + layer * piece
                            part[r * pair + p * piece : r * pair + (p + 1) * piece, cur_at(c)] = (
                                cur[pl.ds(pl.multiple_of(start, piece), piece), cur_at(c)]
                            )
                    else:
                        part[part_at(r), cur_at(c)] = blank

    def part_product(source, i, k):
        low, high = extent(i, k)
        lines = slice((2 * i - depth) * pair, (2 * i - depth + height(i)) * pair)
        inside = slice((low - edge) * tile, (high - edge) * tile)
        product = jnp.dot(
            source[lines, inside],
            cur[inside, (k - edge) * tile : (k - edge + 1) * tile],
            preferred_element_type=jnp.float32,
        )
        for a in range(height(i)):
            for b in range(2):
                r = 2 * i - depth + a
                c = 2 * k - depth + b
                yield r, c, product[a * pair : (a + 1) * pair, b * block : (b + 1) * block]

    def part_squares(i, columns):
        for k in columns:
            for r, c, value in part_product(part, i, k):
                if abs(c - r) <= reach:
                    value = masked(value, r, c - r + reach).astype(jnp.bfloat16)
                else:
                    value = blank
                part_square[part_at(r), cur_at(c)] = value

    def finish(i):
        for k in range(i - span, i + span + 1):
            for r, c, value in part_product(part_square, i, k):
                w = c - r + reach
                if not 0 <= w < band:
                    continue
                before = part[part_at(r), cur_at(c)].astype(jnp.float32)
                after = masked((3.0 * before - value * scale) * 0.5, r, w).astype(jnp.bfloat16)
                o_ref[mirror(r, rows), mirror(w, band)] = after[:piece]
                outbox[r, mirror(w, band)] = after[piece:]

    results = [
        remote(
            outbox.at[r], o_ref.at[mirror(r, rows)], o_send.at[r], o_recv.at[r], (near, g)
        )
        for r in range(half)
    ]
    returned = [
        remote(
            outbox.at[r],
            o_ref.at[mirror(rows - 1 - r, rows)],
            o_send.at[r],
            o_recv.at[r],
            (near, g),
        )
        for r in range(half)
    ]

    exchanges = {}
    partners = {}
    n = 0
    for r in range(half - 1, half - 1 - reach, -1):
        for c in range(rows - half - reach, r + reach + 1):
            there = cur.at[cur_at(rows - 1 - r), cur_at(rows - 1 - c)]
            exchanges[r, c] = remote(
                cur.at[cur_at(r), cur_at(c)], there, c_send.at[n], c_recv.at[n], (near, g)
            )
            partners[r, c] = remote(there, there, c_send.at[n], c_recv.at[n], (near, g))
            n += 1

    def exchange(*rs):
        for r, c in exchanges:
            if r in rs:
                exchanges[r, c].start()

    def forward(*js):
        for j in js:
            for p in range(2):
                arrivals[p, j].wait_recv()
            crossings[j].start()

    def build(*js):
        for j in js:
            landings[j].wait_recv()
            count = min(reach + 1, j + 1)
            r = -1 - j
            for s in range(count):
                c = r + s
                value = masked(halo[j, mirror(s, count)], r, reach + s)
                put(r, c, value)
                if c != r:
                    put(c, r, value.T)

    for t in range(tiles):
        r = 2 * t - depth
        if t + span < tiles:
            put(r, r + reach + 1, empty)
        if t >= span:
            put(r + 1, r - reach, empty)
    for r in range(half, 2 * tiles - depth):
        t = (r + depth) // 2
        for k in range(t - span, min(t + span + 1, tiles)):
            for b in range(2):
                c = 2 * k - depth + b
                if (rows - 1 - r, rows - 1 - c) not in exchanges:
                    cur[cur_at(r), cur_at(c)] = empty

    own_flags.wait()
    for r in order:
        own_rows[r].wait()
        for w in range(band):
            c = r + w - reach
            if c >= 2 * tiles - depth:
                continue
            value = masked(x_ref[mirror(r, rows), mirror(w, band)], r, w)
            put(r, c, value)
            if c < 0:
                put(c, r, value.T)

    pl.semaphore_wait(barrier, len(peers))
    for j in range(depth):
        for side in range(2):
            sends[side, j].start()
        if j == 1:
            flag_copy.start()

    i = last
    squares(i, range(i - span, i + span + 1))
    cubes(i, range(i - span, i + span + 1))
    squares(i - 1, range(i - span, i + 2))
    exchange(half - 1)
    squares(i - 2, range(i - 2, i + 1))
    cubes(i - 1, range(i, i + 2))
    forward(0, 1)
    cubes(i - 2, range(i, i + 1))
    forward(2)
    gather(i)
    flag_copy.wait_recv()
    landed = pltpu.make_async_copy(flags, r2.at[1], local_flags.at[1])
    landed.start()
    landed.wait()
    build(0, 1)
    forward(3)
    squares(i - 1, [i - 3])
    squares(i - 3, [i - 1])
    cubes(i - 1, range(i - 3, i))
    forward(4)
    build(2, 3)
    exchange(half - 2, half - 3)
    squares(i - 2, [i - 4, i - 3])
    squares(i - 3, [i - 2])
    squares(i - 4, [i - 2])
    forward(5)
    cubes(i - 2, range(i - 4, i))
    gather(i - 1)
    gather(i - 2)
    exchange(half - 4)
    forward(6)
    build(4, 5)
    squares(i - 3, range(i - 5, i - 2))
    squares(i - 4, [i - 3])
    for r, c in partners:
        partners[r, c].wait_recv()
    part_squares(i, range(i - span, i + span + 1))
    cubes(i - 3, range(i - 4, i))
    forward(7)
    finish(i)
    part_squares(i - 1, range(i - 3, i + 2))
    results[half - 1].start()
    finish(i - 1)
    part_squares(i - 2, range(i - 1, i + 1))
    results[half - 2].start()
    results[half - 3].start()
    build(6, 7)
    squares(i - 4, range(i - 6, i - 3))
    cubes(i - 4, range(i - 4, i - 1))
    part_squares(i - 2, range(i - 4, i - 1))
    finish(i - 2)
    results[half - 4].start()
    results[half - 5].start()

    for r in range(half):
        returned[r].wait_recv()
    for j in range(depth):
        for side in range(2):
            sends[side, j].wait_send()
        crossings[j].wait_send()
    for key in exchanges:
        exchanges[key].wait_send()
    for r in range(half):
        results[r].wait_send()
    flag_copy.wait_send()


def per_device(layers, grids, band_blocks, retained):
    rows, band, block, _ = band_blocks.shape
    reach = (band - 1) // 2
    depth = 2 * reach
    half = rows // 2
    piece = block // layers
    pair = 2 * piece
    dtype = band_blocks.dtype
    outside = pl.BlockSpec(memory_space=pltpu.HBM)
    tile = 2 * block
    span = reach // 2
    last = (depth + half - 1) // 2
    tiles = last + span + 1
    window = (tiles - reach + span) * tile
    swaps = sum(r + 2 * reach + 1 - rows + half for r in range(half - reach, half))
    dma = pltpu.SemaphoreType.DMA
    return pl.pallas_call(
        functools.partial(purify, (layers, grids, rows, reach, block)),
        out_shape=jax.ShapeDtypeStruct((rows, band, piece, block), dtype),
        in_specs=[outside, outside],
        out_specs=pl.BlockSpec(memory_space=pltpu.VMEM),
        scratch_shapes=[
            pltpu.VMEM((rows, band, block, block), dtype),
            pltpu.VMEM((depth, reach + 1, block, block), dtype),
            pltpu.VMEM((rows, band), retained.dtype),
            pltpu.SMEM((2, rows, band), retained.dtype),
            pltpu.VMEM((tiles * tile, tiles * tile), dtype),
            pltpu.VMEM((window, window), dtype),
            pltpu.VMEM((last - reach + span + 1, tile, (reach + 1) * tile), dtype),
            pltpu.VMEM((half * pair, window), dtype),
            pltpu.VMEM((half * pair, window), dtype),
            pltpu.VMEM((half, band, piece, block), dtype),
            dma((2, depth)),
            dma((2, depth)),
            dma((depth,)),
            dma((depth,)),
            dma((swaps,)),
            dma((swaps,)),
            dma((half,)),
            dma((half,)),
            dma,
            dma,
            dma((rows,)),
            dma((2,)),
        ],
        compiler_params=pltpu.CompilerParams(
            collective_id=0, has_side_effects=True, vmem_limit_bytes=44 * 1024 * 1024
        ),
        name="purify",
    )(band_blocks, retained)


def solution(mesh):
    return jax.shard_map(
        functools.partial(per_device, mesh.shape["layer"], mesh.shape["grid"]),
        mesh=mesh,
        in_specs=(P("grid", None, None, None), P("grid", None)),
        out_specs=P("grid", None, "layer", None),
        check_vma=False,
    )
```

```python
import functools

import jax
import jax.numpy as jnp
from jax import lax
from jax.experimental import pallas as pl
from jax.experimental.pallas import tpu as pltpu
from jax.sharding import PartitionSpec as P

MESH = pl.DeviceIdType.MESH


def purify(dims, x_hbm, r_hbm, o_ref, x_ref, halo, flags, r2, wide, cur, strip, part, part_square,
           outbox, y_send, y_recv, x_send, x_recv, c_send, c_recv, o_send, o_recv, r_send, r_recv,
           local, local_flags, ready):
    layers, grids, rows, reach, block = dims
    piece = block // layers
    pair = 2 * piece
    band = 2 * reach + 1
    depth = 2 * reach
    tile = 2 * block
    span = reach // 2
    half = rows // 2
    scale = 1.0 / (4.0 * band * block)
    last = (depth + half - 1) // 2
    tiles = last + span + 1
    own = reach
    edge = own - span

    q = lax.axis_index("layer")
    g = lax.axis_index("grid")
    core = lax.rem(q, 2)
    base = q - core
    right = lax.rem(g + 1, grids)
    left = lax.rem(g + grids - 1, grids)
    far = lax.rem(q + layers // 2, layers)
    near = base + 1 - core
    outer = jnp.where(core == 0, left, right)
    inner = jnp.where(core == 0, right, left)

    def mirror(i, count):
        return i + core * (count - 1 - 2 * i)

    def strip_of(index, size):
        return pl.ds(pl.multiple_of(index * size, size), size)

    own_flags = pltpu.make_async_copy(r_hbm, r2.at[0], local_flags.at[0])
    own_flags.start()
    order = range(rows)
    own_rows = [
        pltpu.make_async_copy(
            x_hbm.at[mirror(r, rows)], x_ref.at[mirror(r, rows)], local.at[r]
        )
        for r in order
    ]
    for r in order:
        own_rows[r].start()

    barrier = pltpu.get_barrier_semaphore()
    first = g == 0
    final = g == grids - 1
    closing = jnp.logical_and(final, core == 1)
    opening = jnp.logical_and(first, core == 1)

    def signal(semaphore, peer):
        pl.semaphore_signal(semaphore, inc=1, device_id=peer, device_id_type=MESH)

    @pl.when(jnp.logical_not(closing))
    def _():
        signal(barrier, (base, outer))
        signal(barrier, (base + 1, outer))

    @pl.when(opening)
    def _():
        signal(barrier, (base + 1, left))

    signal(barrier, (far, g))
    signal(barrier, (near, g))

    def remote(source, target, send_sem, recv_sem, peer):
        return pltpu.make_async_remote_copy(
            src_ref=source,
            dst_ref=target,
            send_sem=send_sem,
            recv_sem=recv_sem,
            device_id=peer,
            device_id_type=MESH,
        )

    mine = strip_of(q, piece)
    plane = lax.div(q, 2)
    near_rows = strip_of(plane, pair)
    far_rows = strip_of(lax.div(far, 2), pair)
    sides = ((base, right), (base + 1, left))
    sends = {}
    arrivals = {}
    crossings = {}
    landings = {}
    for j in range(depth):
        count = min(reach + 1, j + 1)
        for side in range(2):
            if side == 0:
                source = x_hbm.at[rows - 1 - j, reach : reach + count, mine, :]
            else:
                source = x_hbm.at[j, reach + 1 - count : reach + 1, mine, :]
            there = halo.at[j, 0:count, mine, :]
            sends[side, j] = remote(
                source, there, y_send.at[side, j], y_recv.at[core, j], sides[side]
            )
        for p in range(2):
            here = halo.at[j, 0:count, strip_of(base + p, piece), :]
            arrivals[p, j] = remote(here, here, y_send.at[p, j], y_recv.at[p, j], (near, g))
        across = halo.at[j, 0:count, near_rows, :]
        crossings[j] = remote(across, across, x_send.at[j], x_recv.at[j], (far, g))
        beyond = halo.at[j, 0:count, far_rows, :]
        landings[j] = remote(beyond, beyond, x_send.at[j], x_recv.at[j], (far, g))
    flag_copy = remote(r_hbm, flags, r_send, r_recv, (q, inner))

    def at(r):
        return slice((r + depth) * block, (r + depth + 1) * block)

    def cur_at(r):
        return slice((r + reach) * block, (r + reach + 1) * block)

    def masked(value, r, w):
        kept = r2[0 if r >= 0 else 1, mirror(r % rows, rows), mirror(w, band)]
        return jnp.where(kept != 0, value, jnp.zeros_like(value))

    def put(r, c, value):
        wide[at(r), at(c)] = value

    empty = jnp.zeros((block, block), jnp.bfloat16)
    blank = jnp.zeros((pair, block), jnp.bfloat16)

    def height(i):
        return min(2, depth + half - 2 * i)

    def extent(i, c):
        return max(i, c) - span, min(i, c) + span + 1

    def squares(i, columns):
        m = height(i)
        lines = slice(i * tile, i * tile + m * block)
        for c in columns:
            low, high = extent(i, c)
            product = jnp.dot(
                wide[lines, low * tile : high * tile],
                wide[low * tile : high * tile, c * tile : (c + 1) * tile],
                preferred_element_type=jnp.float32,
            )
            for a in range(m):
                for b in range(2):
                    w = 2 * (c - i) + b - a + reach
                    if 0 <= w < band:
                        value = masked(
                            product[a * block : (a + 1) * block, b * block : (b + 1) * block],
                            2 * i - depth + a,
                            w,
                        ).astype(jnp.bfloat16)
                    else:
                        value = empty
                    to = (c - i + span) * tile + b * block
                    strip[i - edge, a * block : (a + 1) * block, to : to + block] = value

    def cubes(i, columns):
        m = height(i)
        lines = slice(i * tile, i * tile + m * block)
        for k in columns:
            low, high = extent(i, k)
            product = jnp.dot(
                strip[
                    i - edge, 0 : m * block, (low - i + span) * tile : (high - i + span) * tile
                ],
                wide[low * tile : high * tile, k * tile : (k + 1) * tile],
                preferred_element_type=jnp.float32,
            )
            before = wide[lines, k * tile : (k + 1) * tile].astype(jnp.float32)
            after = (3.0 * before - product * scale) * 0.5
            for a in range(m):
                r = 2 * i - depth + a
                for b in range(2):
                    c = 2 * k - depth + b
                    w = c - r + reach
                    if 0 <= w < band:
                        value = masked(
                            after[a * block : (a + 1) * block, b * block : (b + 1) * block], r, w
                        ).astype(jnp.bfloat16)
                    else:
                        value = empty
                    cur[cur_at(r), cur_at(c)] = value

    def part_at(r):
        return slice(r * pair, (r + 1) * pair)

    def gather(i):
        for a in range(height(i)):
            r = 2 * i - depth + a
            for k in range(i - span, i + span + 1):
                for b in range(2):
                    c = 2 * k - depth + b
                    if abs(c - r) <= reach:
                        for p, layer in enumerate((q, near)):
                            start = (r + reach) * block + layer * piece
                            part[r * pair + p * piece : r * pair + (p + 1) * piece, cur_at(c)] = (
                                cur[pl.ds(pl.multiple_of(start, piece), piece), cur_at(c)]
                            )
                    else:
                        part[part_at(r), cur_at(c)] = blank

    def part_product(source, i, k):
        low, high = extent(i, k)
        lines = slice((2 * i - depth) * pair, (2 * i - depth + height(i)) * pair)
        inside = slice((low - edge) * tile, (high - edge) * tile)
        product = jnp.dot(
            source[lines, inside],
            cur[inside, (k - edge) * tile : (k - edge + 1) * tile],
            preferred_element_type=jnp.float32,
        )
        for a in range(height(i)):
            for b in range(2):
                r = 2 * i - depth + a
                c = 2 * k - depth + b
                yield r, c, product[a * pair : (a + 1) * pair, b * block : (b + 1) * block]

    def part_squares(i, columns):
        for k in columns:
            for r, c, value in part_product(part, i, k):
                if abs(c - r) <= reach:
                    value = masked(value, r, c - r + reach).astype(jnp.bfloat16)
                else:
                    value = blank
                part_square[part_at(r), cur_at(c)] = value

    def finish(i):
        for k in range(i - span, i + span + 1):
            for r, c, value in part_product(part_square, i, k):
                w = c - r + reach
                if not 0 <= w < band:
                    continue
                before = part[part_at(r), cur_at(c)].astype(jnp.float32)
                after = masked((3.0 * before - value * scale) * 0.5, r, w).astype(jnp.bfloat16)
                o_ref[mirror(r, rows), mirror(w, band)] = after[:piece]
                outbox[r, mirror(w, band)] = after[piece:]

    results = [
        remote(
            outbox.at[r], o_ref.at[mirror(r, rows)], o_send.at[r], o_recv.at[r], (near, g)
        )
        for r in range(half)
    ]
    returned = [
        remote(
            outbox.at[r],
            o_ref.at[mirror(rows - 1 - r, rows)],
            o_send.at[r],
            o_recv.at[r],
            (near, g),
        )
        for r in range(half)
    ]

    exchanges = {}
    partners = {}
    n = 0
    for r in range(half - 1, half - 1 - reach, -1):
        for c in range(rows - half - reach, r + reach + 1):
            there = cur.at[cur_at(rows - 1 - r), cur_at(rows - 1 - c)]
            exchanges[r, c] = remote(
                cur.at[cur_at(r), cur_at(c)], there, c_send.at[n], c_recv.at[n], (near, g)
            )
            partners[r, c] = remote(there, there, c_send.at[n], c_recv.at[n], (near, g))
            n += 1

    def exchange(*rs):
        for r, c in exchanges:
            if r in rs:
                exchanges[r, c].start()

    def forward(*js):
        for j in js:
            for p in range(2):
                arrivals[p, j].wait_recv()
            crossings[j].start()

    def build(*js):
        for j in js:
            landings[j].wait_recv()
            count = min(reach + 1, j + 1)
            r = -1 - j
            for s in range(count):
                c = r + s
                value = masked(halo[j, mirror(s, count)], r, reach + s)
                put(r, c, value)
                if c != r:
                    put(c, r, value.T)

    for t in range(tiles):
        r = 2 * t - depth
        if t + span < tiles:
            put(r, r + reach + 1, empty)
        if t >= span:
            put(r + 1, r - reach, empty)
    for r in range(half, 2 * tiles - depth):
        t = (r + depth) // 2
        for k in range(t - span, min(t + span + 1, tiles)):
            for b in range(2):
                c = 2 * k - depth + b
                if (rows - 1 - r, rows - 1 - c) not in exchanges:
                    cur[cur_at(r), cur_at(c)] = empty

    pl.semaphore_wait(barrier, 4 + closing.astype(jnp.int32) - first.astype(jnp.int32))

    @pl.when(closing)
    def _():
        signal(ready, (base, right))
        signal(ready, (base + 1, right))

    @pl.when(jnp.logical_or(first, final))
    def _():
        for j in range(depth):
            sends[0, j].start()

    @pl.when(final)
    def _():
        for j in range(depth):
            sends[1, j].start()

    @pl.when(jnp.logical_not(jnp.logical_or(first, final)))
    def _():
        for j in range(depth):
            for side in range(2):
                sends[side, j].start()

    @pl.when(jnp.logical_not(opening))
    def _():
        flag_copy.start()

    own_flags.wait()
    for r in order:
        own_rows[r].wait()
        for w in range(band):
            c = r + w - reach
            if c >= 2 * tiles - depth:
                continue
            value = masked(x_ref[mirror(r, rows), mirror(w, band)], r, w)
            put(r, c, value)
            if c < 0:
                put(c, r, value.T)


    i = last
    squares(i, range(i - span, i + span + 1))
    cubes(i, range(i - span, i + span + 1))

    @pl.when(first)
    def _():
        pl.semaphore_wait(ready, 1)
        for j in range(depth):
            sends[1, j].start()

    @pl.when(opening)
    def _():
        flag_copy.start()

    forward(0, 1)
    squares(i - 1, range(i - span, i + 2))
    exchange(half - 1)
    forward(2)
    squares(i - 2, range(i - 2, i + 1))
    cubes(i - 1, range(i, i + 2))
    cubes(i - 2, range(i, i + 1))
    gather(i)
    forward(3)
    flag_copy.wait_recv()
    landed = pltpu.make_async_copy(flags, r2.at[1], local_flags.at[1])
    landed.start()
    landed.wait()
    build(0, 1)
    squares(i - 1, [i - 3])
    squares(i - 3, [i - 1])
    forward(4)
    cubes(i - 1, range(i - 3, i))
    exchange(half - 2, half - 3)
    forward(5)
    build(2, 3)
    squares(i - 2, [i - 4, i - 3])
    squares(i - 3, [i - 2])
    squares(i - 4, [i - 2])
    cubes(i - 2, range(i - 4, i))
    gather(i - 1)
    gather(i - 2)
    exchange(half - 4)
    forward(6)
    for r, c in partners:
        partners[r, c].wait_recv()
    part_squares(i, range(i - span, i + span + 1))
    forward(7)
    finish(i)
    results[half - 1].start()
    build(4, 5)
    squares(i - 3, range(i - 5, i - 2))
    squares(i - 4, [i - 3])
    cubes(i - 3, range(i - 4, i))
    part_squares(i - 1, range(i - 3, i + 2))
    finish(i - 1)
    part_squares(i - 2, range(i - 1, i + 1))
    results[half - 2].start()
    results[half - 3].start()
    build(6, 7)
    squares(i - 4, range(i - 6, i - 3))
    cubes(i - 4, range(i - 4, i - 1))
    part_squares(i - 2, range(i - 4, i - 1))
    finish(i - 2)
    results[half - 4].start()
    results[half - 5].start()

    for r in range(half):
        returned[r].wait_recv()
    for j in range(depth):
        for side in range(2):
            sends[side, j].wait_send()
        crossings[j].wait_send()
    for key in exchanges:
        exchanges[key].wait_send()
    for r in range(half):
        results[r].wait_send()
    flag_copy.wait_send()


def per_device(layers, grids, band_blocks, retained):
    rows, band, block, _ = band_blocks.shape
    reach = (band - 1) // 2
    depth = 2 * reach
    half = rows // 2
    piece = block // layers
    pair = 2 * piece
    dtype = band_blocks.dtype
    outside = pl.BlockSpec(memory_space=pltpu.HBM)
    tile = 2 * block
    span = reach // 2
    last = (depth + half - 1) // 2
    tiles = last + span + 1
    window = (tiles - reach + span) * tile
    swaps = sum(r + 2 * reach + 1 - rows + half for r in range(half - reach, half))
    dma = pltpu.SemaphoreType.DMA
    return pl.pallas_call(
        functools.partial(purify, (layers, grids, rows, reach, block)),
        out_shape=jax.ShapeDtypeStruct((rows, band, piece, block), dtype),
        in_specs=[outside, outside],
        out_specs=pl.BlockSpec(memory_space=pltpu.VMEM),
        scratch_shapes=[
            pltpu.VMEM((rows, band, block, block), dtype),
            pltpu.VMEM((depth, reach + 1, block, block), dtype),
            pltpu.VMEM((rows, band), retained.dtype),
            pltpu.SMEM((2, rows, band), retained.dtype),
            pltpu.VMEM((tiles * tile, tiles * tile), dtype),
            pltpu.VMEM((window, window), dtype),
            pltpu.VMEM((last - reach + span + 1, tile, (reach + 1) * tile), dtype),
            pltpu.VMEM((half * pair, window), dtype),
            pltpu.VMEM((half * pair, window), dtype),
            pltpu.VMEM((half, band, piece, block), dtype),
            dma((2, depth)),
            dma((2, depth)),
            dma((depth,)),
            dma((depth,)),
            dma((swaps,)),
            dma((swaps,)),
            dma((half,)),
            dma((half,)),
            dma,
            dma,
            dma((rows,)),
            dma((2,)),
            pltpu.SemaphoreType.REGULAR,
        ],
        compiler_params=pltpu.CompilerParams(
            collective_id=0, has_side_effects=True, vmem_limit_bytes=44 * 1024 * 1024
        ),
        name="purify",
    )(pltpu.with_memory_space_constraint(band_blocks, pltpu.HBM), pltpu.with_memory_space_constraint(retained, pltpu.HBM))


def solution(mesh):
    return jax.shard_map(
        functools.partial(per_device, mesh.shape["layer"], mesh.shape["grid"]),
        mesh=mesh,
        in_specs=(P("grid", None, None, None), P("grid", None)),
        out_specs=P("grid", None, "layer", None),
        check_vma=False,
    )
```

```python
import functools

import jax
import jax.numpy as jnp
from jax import lax
from jax.experimental import pallas as pl
from jax.experimental.pallas import tpu as pltpu
from jax.sharding import PartitionSpec as P

MESH = pl.DeviceIdType.MESH


def purify(dims, x_hbm, r_hbm, o_ref, x_ref, halo, flags, r2, wide, cur, strip, part, part_square,
           outbox, y_send, y_recv, x_send, x_recv, c_send, c_recv, o_send, o_recv, r_send, r_recv,
           local, local_flags, ready):
    layers, grids, rows, reach, block = dims
    piece = block // layers
    pair = 2 * piece
    band = 2 * reach + 1
    depth = 2 * reach
    tile = 2 * block
    span = reach // 2
    half = rows // 2
    scale = 1.0 / (4.0 * band * block)
    last = (depth + half - 1) // 2
    tiles = last + span + 1
    own = reach
    edge = own - span

    q = lax.axis_index("layer")
    g = lax.axis_index("grid")
    core = lax.rem(q, 2)
    base = q - core
    right = lax.rem(g + 1, grids)
    left = lax.rem(g + grids - 1, grids)
    far = lax.rem(q + layers // 2, layers)
    near = base + 1 - core
    outer = jnp.where(core == 0, left, right)
    inner = jnp.where(core == 0, right, left)

    def mirror(i, count):
        return i + core * (count - 1 - 2 * i)

    def strip_of(index, size):
        return pl.ds(pl.multiple_of(index * size, size), size)

    own_flags = pltpu.make_async_copy(r_hbm, r2.at[0], local_flags.at[0])
    own_flags.start()
    order = range(rows)
    own_rows = [
        pltpu.make_async_copy(
            x_hbm.at[mirror(r, rows)], x_ref.at[mirror(r, rows)], local.at[r]
        )
        for r in order
    ]
    for r in order:
        own_rows[r].start()

    barrier = pltpu.get_barrier_semaphore()
    first = g == 0
    final = g == grids - 1
    closing = jnp.logical_and(final, core == 1)
    opening = jnp.logical_and(first, core == 1)

    def signal(semaphore, peer):
        pl.semaphore_signal(semaphore, inc=1, device_id=peer, device_id_type=MESH)

    @pl.when(jnp.logical_not(closing))
    def _():
        signal(barrier, (base, outer))
        signal(barrier, (base + 1, outer))

    @pl.when(opening)
    def _():
        signal(barrier, (base + 1, left))

    signal(barrier, (far, g))
    signal(barrier, (near, g))

    def remote(source, target, send_sem, recv_sem, peer):
        return pltpu.make_async_remote_copy(
            src_ref=source,
            dst_ref=target,
            send_sem=send_sem,
            recv_sem=recv_sem,
            device_id=peer,
            device_id_type=MESH,
        )

    mine = strip_of(q, piece)
    plane = lax.div(q, 2)
    near_rows = strip_of(plane, pair)
    far_rows = strip_of(lax.div(far, 2), pair)
    sides = ((base, right), (base + 1, left))
    sends = {}
    arrivals = {}
    crossings = {}
    landings = {}
    for j in range(depth):
        count = min(reach + 1, j + 1)
        for side in range(2):
            if side == 0:
                source = x_hbm.at[rows - 1 - j, reach : reach + count, mine, :]
            else:
                source = x_hbm.at[j, reach + 1 - count : reach + 1, mine, :]
            there = halo.at[j, 0:count, mine, :]
            sends[side, j] = remote(
                source, there, y_send.at[side, j], y_recv.at[core, j], sides[side]
            )
        for p in range(2):
            here = halo.at[j, 0:count, strip_of(base + p, piece), :]
            arrivals[p, j] = remote(here, here, y_send.at[p, j], y_recv.at[p, j], (near, g))
        across = halo.at[j, 0:count, near_rows, :]
        crossings[j] = remote(across, across, x_send.at[j], x_recv.at[j], (far, g))
        beyond = halo.at[j, 0:count, far_rows, :]
        landings[j] = remote(beyond, beyond, x_send.at[j], x_recv.at[j], (far, g))
    flag_copy = remote(r_hbm, flags, r_send, r_recv, (q, inner))

    def at(r):
        return slice((r + depth) * block, (r + depth + 1) * block)

    def cur_at(r):
        return slice((r + reach) * block, (r + reach + 1) * block)

    def masked(value, r, w):
        kept = r2[0 if r >= 0 else 1, mirror(r % rows, rows), mirror(w, band)]
        return jnp.where(kept != 0, value, jnp.zeros_like(value))

    def put(r, c, value):
        wide[at(r), at(c)] = value

    empty = jnp.zeros((block, block), jnp.bfloat16)
    blank = jnp.zeros((pair, block), jnp.bfloat16)

    def height(i):
        return min(2, depth + half - 2 * i)

    def extent(i, c):
        return max(i, c) - span, min(i, c) + span + 1

    def squares(i, columns):
        m = height(i)
        lines = slice(i * tile, i * tile + m * block)
        for c in columns:
            low, high = extent(i, c)
            product = jnp.dot(
                wide[lines, low * tile : high * tile],
                wide[low * tile : high * tile, c * tile : (c + 1) * tile],
                preferred_element_type=jnp.float32,
            )
            for a in range(m):
                for b in range(2):
                    w = 2 * (c - i) + b - a + reach
                    if 0 <= w < band:
                        value = masked(
                            product[a * block : (a + 1) * block, b * block : (b + 1) * block],
                            2 * i - depth + a,
                            w,
                        ).astype(jnp.bfloat16)
                    else:
                        value = empty
                    to = (c - i + span) * tile + b * block
                    strip[i - edge, a * block : (a + 1) * block, to : to + block] = value

    def cubes(i, columns):
        m = height(i)
        lines = slice(i * tile, i * tile + m * block)
        for k in columns:
            low, high = extent(i, k)
            product = jnp.dot(
                strip[
                    i - edge, 0 : m * block, (low - i + span) * tile : (high - i + span) * tile
                ],
                wide[low * tile : high * tile, k * tile : (k + 1) * tile],
                preferred_element_type=jnp.float32,
            )
            before = wide[lines, k * tile : (k + 1) * tile].astype(jnp.float32)
            after = (3.0 * before - product * scale) * 0.5
            for a in range(m):
                r = 2 * i - depth + a
                for b in range(2):
                    c = 2 * k - depth + b
                    w = c - r + reach
                    if 0 <= w < band:
                        value = masked(
                            after[a * block : (a + 1) * block, b * block : (b + 1) * block], r, w
                        ).astype(jnp.bfloat16)
                    else:
                        value = empty
                    cur[cur_at(r), cur_at(c)] = value

    def part_at(r):
        return slice(r * pair, (r + 1) * pair)

    def gather(i):
        for a in range(height(i)):
            r = 2 * i - depth + a
            for k in range(i - span, i + span + 1):
                for b in range(2):
                    c = 2 * k - depth + b
                    if abs(c - r) <= reach:
                        for p, layer in enumerate((q, near)):
                            start = (r + reach) * block + layer * piece
                            part[r * pair + p * piece : r * pair + (p + 1) * piece, cur_at(c)] = (
                                cur[pl.ds(pl.multiple_of(start, piece), piece), cur_at(c)]
                            )
                    else:
                        part[part_at(r), cur_at(c)] = blank

    def part_product(source, i, k):
        low, high = extent(i, k)
        lines = slice((2 * i - depth) * pair, (2 * i - depth + height(i)) * pair)
        inside = slice((low - edge) * tile, (high - edge) * tile)
        product = jnp.dot(
            source[lines, inside],
            cur[inside, (k - edge) * tile : (k - edge + 1) * tile],
            preferred_element_type=jnp.float32,
        )
        for a in range(height(i)):
            for b in range(2):
                r = 2 * i - depth + a
                c = 2 * k - depth + b
                yield r, c, product[a * pair : (a + 1) * pair, b * block : (b + 1) * block]

    def part_squares(i, columns):
        for k in columns:
            for r, c, value in part_product(part, i, k):
                if abs(c - r) <= reach:
                    value = masked(value, r, c - r + reach).astype(jnp.bfloat16)
                else:
                    value = blank
                part_square[part_at(r), cur_at(c)] = value

    def finish(i):
        for k in range(i - span, i + span + 1):
            for r, c, value in part_product(part_square, i, k):
                w = c - r + reach
                if not 0 <= w < band:
                    continue
                before = part[part_at(r), cur_at(c)].astype(jnp.float32)
                after = masked((3.0 * before - value * scale) * 0.5, r, w).astype(jnp.bfloat16)
                o_ref[mirror(r, rows), mirror(w, band)] = after[:piece]
                outbox[r, mirror(w, band)] = after[piece:]

    results = [
        remote(
            outbox.at[r], o_ref.at[mirror(r, rows)], o_send.at[r], o_recv.at[r], (near, g)
        )
        for r in range(half)
    ]
    returned = [
        remote(
            outbox.at[r],
            o_ref.at[mirror(rows - 1 - r, rows)],
            o_send.at[r],
            o_recv.at[r],
            (near, g),
        )
        for r in range(half)
    ]

    exchanges = {}
    partners = {}
    n = 0
    for r in range(half - 1, half - 1 - reach, -1):
        for c in range(rows - half - reach, r + reach + 1):
            there = cur.at[cur_at(rows - 1 - r), cur_at(rows - 1 - c)]
            exchanges[r, c] = remote(
                cur.at[cur_at(r), cur_at(c)], there, c_send.at[n], c_recv.at[n], (near, g)
            )
            partners[r, c] = remote(there, there, c_send.at[n], c_recv.at[n], (near, g))
            n += 1

    def exchange(*rs):
        for r, c in exchanges:
            if r in rs:
                exchanges[r, c].start()

    def forward(*js):
        for j in js:
            for p in range(2):
                arrivals[p, j].wait_recv()
            crossings[j].start()

    def build(*js):
        for j in js:
            landings[j].wait_recv()
            count = min(reach + 1, j + 1)
            r = -1 - j
            for s in range(count):
                c = r + s
                value = masked(halo[j, mirror(s, count)], r, reach + s)
                put(r, c, value)
                if c != r:
                    put(c, r, value.T)

    for t in range(tiles):
        r = 2 * t - depth
        if t + span < tiles:
            put(r, r + reach + 1, empty)
        if t >= span:
            put(r + 1, r - reach, empty)
    for r in range(half, 2 * tiles - depth):
        t = (r + depth) // 2
        for k in range(t - span, min(t + span + 1, tiles)):
            for b in range(2):
                c = 2 * k - depth + b
                if (rows - 1 - r, rows - 1 - c) not in exchanges:
                    cur[cur_at(r), cur_at(c)] = empty

    pl.semaphore_wait(barrier, 4 + closing.astype(jnp.int32) - first.astype(jnp.int32))

    @pl.when(closing)
    def _():
        signal(ready, (base, right))
        signal(ready, (base + 1, right))

    @pl.when(jnp.logical_not(opening))
    def _():
        flag_copy.start()

    @pl.when(jnp.logical_or(first, final))
    def _():
        for j in range(depth):
            sends[0, j].start()

    @pl.when(final)
    def _():
        for j in range(depth):
            sends[1, j].start()

    @pl.when(jnp.logical_not(jnp.logical_or(first, final)))
    def _():
        for j in range(depth):
            for side in range(2):
                sends[side, j].start()

    own_flags.wait()
    for r in order:
        own_rows[r].wait()
        for w in range(band):
            c = r + w - reach
            if c >= 2 * tiles - depth:
                continue
            value = masked(x_ref[mirror(r, rows), mirror(w, band)], r, w)
            put(r, c, value)
            if c < 0:
                put(c, r, value.T)


    i = last
    squares(i, range(i - span, i + span + 1))
    cubes(i, range(i - span, i + span + 1))

    @pl.when(first)
    def _():
        pl.semaphore_wait(ready, 1)

        @pl.when(core == 1)
        def _():
            flag_copy.start()

        for j in range(depth):
            sends[1, j].start()

    forward(0, 1)
    squares(i - 1, range(i - span, i + 2))
    exchange(half - 1)
    forward(2)
    squares(i - 2, range(i - 2, i + 1))
    cubes(i - 1, range(i, i + 2))
    cubes(i - 2, range(i, i + 1))
    gather(i)
    forward(3)
    flag_copy.wait_recv()
    landed = pltpu.make_async_copy(flags, r2.at[1], local_flags.at[1])
    landed.start()
    landed.wait()
    build(0, 1)
    squares(i - 1, [i - 3])
    squares(i - 3, [i - 1])
    forward(4)
    cubes(i - 1, range(i - 3, i))
    exchange(half - 2, half - 3)
    forward(5)
    build(2, 3)
    squares(i - 2, [i - 4, i - 3])
    squares(i - 3, [i - 2])
    squares(i - 4, [i - 2])
    cubes(i - 2, range(i - 4, i))
    gather(i - 1)
    gather(i - 2)
    exchange(half - 4)
    forward(6)
    for r, c in partners:
        partners[r, c].wait_recv()
    part_squares(i, range(i - span, i + span + 1))
    forward(7)
    finish(i)
    results[half - 1].start()
    build(4, 5)
    squares(i - 3, range(i - 5, i - 2))
    squares(i - 4, [i - 3])
    cubes(i - 3, range(i - 4, i))
    part_squares(i - 1, range(i - 3, i + 2))
    finish(i - 1)
    part_squares(i - 2, range(i - 1, i + 1))
    results[half - 2].start()
    results[half - 3].start()
    build(6, 7)
    squares(i - 4, range(i - 6, i - 3))
    cubes(i - 4, range(i - 4, i - 1))
    part_squares(i - 2, range(i - 4, i - 1))
    finish(i - 2)
    results[half - 4].start()
    results[half - 5].start()

    for r in range(half):
        returned[r].wait_recv()
    for j in range(depth):
        for side in range(2):
            sends[side, j].wait_send()
        crossings[j].wait_send()
    for key in exchanges:
        exchanges[key].wait_send()
    for r in range(half):
        results[r].wait_send()
    flag_copy.wait_send()


def per_device(layers, grids, band_blocks, retained):
    rows, band, block, _ = band_blocks.shape
    reach = (band - 1) // 2
    depth = 2 * reach
    half = rows // 2
    piece = block // layers
    pair = 2 * piece
    dtype = band_blocks.dtype
    outside = pl.BlockSpec(memory_space=pltpu.HBM)
    tile = 2 * block
    span = reach // 2
    last = (depth + half - 1) // 2
    tiles = last + span + 1
    window = (tiles - reach + span) * tile
    swaps = sum(r + 2 * reach + 1 - rows + half for r in range(half - reach, half))
    dma = pltpu.SemaphoreType.DMA
    return pl.pallas_call(
        functools.partial(purify, (layers, grids, rows, reach, block)),
        out_shape=jax.ShapeDtypeStruct((rows, band, piece, block), dtype),
        in_specs=[outside, outside],
        out_specs=pl.BlockSpec(memory_space=pltpu.VMEM),
        scratch_shapes=[
            pltpu.VMEM((rows, band, block, block), dtype),
            pltpu.VMEM((depth, reach + 1, block, block), dtype),
            pltpu.VMEM((rows, band), retained.dtype),
            pltpu.SMEM((2, rows, band), retained.dtype),
            pltpu.VMEM((tiles * tile, tiles * tile), dtype),
            pltpu.VMEM((window, window), dtype),
            pltpu.VMEM((last - reach + span + 1, tile, (reach + 1) * tile), dtype),
            pltpu.VMEM((half * pair, window), dtype),
            pltpu.VMEM((half * pair, window), dtype),
            pltpu.VMEM((half, band, piece, block), dtype),
            dma((2, depth)),
            dma((2, depth)),
            dma((depth,)),
            dma((depth,)),
            dma((swaps,)),
            dma((swaps,)),
            dma((half,)),
            dma((half,)),
            dma,
            dma,
            dma((rows,)),
            dma((2,)),
            pltpu.SemaphoreType.REGULAR,
        ],
        compiler_params=pltpu.CompilerParams(
            collective_id=0, has_side_effects=True, vmem_limit_bytes=44 * 1024 * 1024
        ),
        name="purify",
    )(pltpu.with_memory_space_constraint(band_blocks, pltpu.HBM), pltpu.with_memory_space_constraint(retained, pltpu.HBM))


def solution(mesh):
    return jax.shard_map(
        functools.partial(per_device, mesh.shape["layer"], mesh.shape["grid"]),
        mesh=mesh,
        in_specs=(P("grid", None, None, None), P("grid", None)),
        out_specs=P("grid", None, "layer", None),
        check_vma=False,
    )
```
